256 devices in a mesh: row: 32 (over x, z_hi, core), col: 8 (over y, z_lo).
Axes of the slice: x: 4, y: 4, z: 8 (z_hi: 4, z_lo: 2; z = z_hi * 2 + z_lo), core: 2. Of those that a mesh axis runs over, the one named last changes fastest.
Arguments:
- ancestor_inverse: float32 [6, 32, 24, 8, 128, 128], P(None, 'row', None, 'col'), may hold values from -6 to 6
- block_pattern: int32 [192, 192], replicated, may hold values 0 or 1
- ancestor_lists: int32 [16, 160], replicated, may hold values from 0 to 191, as said below
- panel: float32 [24, 8, 128, 1024], P(None, 'col', 'row'), may hold values from -0.109375 to 0.109375
- diag_term: float32 [16, 64, 64], P('col'), may hold values from -6 to 6
Outputs:
- solved: float32 [6, 32, 128, 1024], P(None, 'row', None, 'col')
- diagonal: float32 [16, 64, 64], P('col')
The draws below stay inside these ranges and needn't reach their ends.
Inputs may be any that keep to these rules, and one draw needn't show every extreme that they name: `ancestor_lists`: each row names 160 different block rows; block 191 is in every row.
All inputs are finite; a program needn't handle non-finite values.
Results may differ from the reference program's by a relative error of at most 0.00007.
Values sent between devices are 32-bit elements; how exact they have to be, the bound alone decides.
A program may use at most 128 MiB of HBM per device.

```python
import jax
import jax.numpy as jnp
from jax import lax

NB = 192
BS = 128
W = 64
NSUP = 16
M = 160
RB = 6
CB = 24
COLS = 1024
N_ROW = 32
N_COL = 8


def draw_ancestor_lists(key, part):
    keys = jax.random.split(jax.random.fold_in(key, 11), NSUP)
    orders = jax.vmap(lambda one_key: jax.random.permutation(one_key, NB - 1))(keys).astype(jnp.int32)
    first_row = orders[0]
    leading = first_row[0]
    first_row = jnp.where(first_row == 0, leading, first_row)
    first_row = first_row.at[0].set(0)
    orders = orders.at[0].set(first_row)
    last_block = jnp.full((NSUP, 1), NB - 1, jnp.int32)
    return jnp.concatenate([orders[:, :M - 1], last_block], axis=1).astype(jnp.int32)


def with_ends(drawn, key, low, top_value):
    shape = drawn.shape
    place = [jax.random.randint(jax.random.fold_in(key, axis), (), 0, shape[axis]) for axis in range(len(shape))]
    drawn = drawn.at[tuple(place)].set(low)
    longest = shape.index(max(shape))
    place[longest] = (place[longest] + 1) % shape[longest]
    return drawn.at[tuple(place)].set(top_value)


def block_scale(own_key, dims, shards, smallest, largest):
    def one(dim, shards_of):
        draws = jax.random.uniform(jax.random.fold_in(jax.random.fold_in(own_key, 6), dim), (shards_of,), jnp.float32, smallest / len(shards), largest / len(shards))
        return jnp.repeat(jnp.exp(draws), dims[dim] // shards_of).reshape((-1,) + (1,) * (len(dims) - dim - 1))

    level = one(*shards[0])
    for cut in shards[1:]:
        level = level * one(*cut)
    return level


def normal_values(stream_key, dims, width, limit, shards=(), kind=jnp.bfloat16):
    array = width * jax.random.normal(stream_key, dims, jnp.float32)
    if shards:
        array = array * block_scale(stream_key, dims, shards, -0.22, 0.18)
    return jnp.clip(array, -limit, limit).astype(kind)


def setup_inputs(seed: int = 0) -> dict:
    splits = jax.random.split(jax.random.key(seed), 6)
    return {
        "ancestor_inverse": normal_values(splits[0], (RB, N_ROW, CB, N_COL, BS, BS), 1.0, 6.0, ((1, 32), (3, 8)), jnp.float32),
        "block_pattern": with_ends((jax.random.randint(splits[1], (NB, NB), 0, 8) < 7).astype(jnp.int32), jax.random.fold_in(splits[1], 1), 0, 1),
        "ancestor_lists": draw_ancestor_lists(jax.random.fold_in(splits[5], 71), 0),
        "panel": normal_values(splits[3], (CB, N_COL, BS, COLS), 0.007, 0.109375, ((1, 8), (2, 32)), jnp.float32),
        "diag_term": normal_values(splits[4], (NSUP, W, W), 1.0, 6.0, ((0, 8),), jnp.float32),
    }


def reference(ancestor_inverse, block_pattern, ancestor_lists, panel, diag_term):
    columns = NSUP * W
    member = jnp.any(ancestor_lists[:, :, None] == jnp.arange(NB, dtype=jnp.int32)[None, None, :], axis=1).astype(jnp.float32)
    block_member = jnp.repeat(member.T, W, axis=1)
    blocks = ancestor_inverse.reshape(NB, NB, BS, BS)
    factors = panel.reshape(NB, BS, columns) * block_member[:, None, :]
    pattern = block_pattern.astype(jnp.float32)

    def one_row(index):
        row_blocks = blocks[index] * pattern[index][:, None, None]
        summed = jnp.einsum("cxy,cyk->xk", row_blocks, factors, precision=lax.Precision.HIGHEST, preferred_element_type=jnp.float32)
        return -summed * block_member[index][None, :]

    solved = lax.map(one_row, jnp.arange(NB, dtype=jnp.int32))
    products = jnp.einsum("bxsi,bxsj->sij", factors.reshape(NB, BS, NSUP, W), solved.reshape(NB, BS, NSUP, W), precision=lax.Precision.HIGHEST, preferred_element_type=jnp.float32)
    diagonal = diag_term - products
    return solved.reshape(NB // N_ROW, N_ROW, BS, columns), diagonal
```

```python
import jax
import jax.numpy as jnp
from jax import lax
from jax.experimental import pallas as pl
from jax.experimental.pallas import tpu as pltpu
from jax.sharding import PartitionSpec as P

NX, NH, NC, NY, NZ = 4, 4, 2, 4, 2
NCHUNK = 4
RBL, CBL, BS = 6, 24, 128
SLICE = RBL * BS // NY
F32, BF16 = jnp.float32, jnp.bfloat16
NT = (((1,), (1,)), ((), ()))
TN = (((0,), (0,)), ((), ()))


def split(value):
    high = value.astype(BF16)
    return high, (value - high.astype(F32)).astype(BF16)


def iota(shape, dim):
    return lax.broadcasted_iota(jnp.int32, shape, dim)


def kernel(panel, s_hbm, pat, lists, diag, solved, diag_out,
           G, SB, S32, Shi, Slo, Lhi, Llo, O, YR, T, ZR, FB, XB, MIR, MC, RM, PM, DA, DX, DH,
           s_sem, sib_s, sib_r, R, zs, xs, xf, fs, fr, ys, yr, ws, wr, gs, gr, ms, mr, ds_s, ds_r):
    row, col = lax.axis_index("row"), lax.axis_index("col")
    x, h, c = row // 8, (row // 2) % 4, row % 2
    y, zl = col // 2, col % 2

    def dev(xx=x, hh=h, cc=c, yy=y, zz=zl):
        return (xx * 8 + hh * 2 + cc, yy * 2 + zz)

    def rcopy(src, dst, send, recv, device):
        return pltpu.make_async_remote_copy(src_ref=src, dst_ref=dst, send_sem=send, recv_sem=recv,
                                            device_id=device, device_id_type=pl.DeviceIdType.MESH)

    sibling = dev(cc=1 - c)
    xp, xm, x2 = (x + 1) % 4, (x + 3) % 4, (x + 2) % 4
    barrier = pltpu.get_barrier_semaphore()
    partners = [sibling]
    partners += [dev(xx=(x + d) % 4) for d in (1, 2, 3)]
    partners += [dev(hh=(h + d) % 4) for d in (1, 2, 3)]
    partners += [(row, (col + d) % 8) for d in range(1, 8)]
    for partner in partners:
        pl.semaphore_signal(barrier, inc=1, device_id=partner, device_id_type=pl.DeviceIdType.MESH)

    loads = [pltpu.make_async_copy(s_hbm.at[a, 0, :, 0], S32.at[a], s_sem.at[a]) for a in range(RBL)]
    for load in loads:
        load.start()
    pl.semaphore_wait(barrier, len(partners))

    sends = []

    def go(copy):
        copy.start()
        sends.append(copy)

    swaps = []
    for k in range(NCHUNK):
        away = pl.multiple_of((2 * k + 1 - c) * BS, BS)
        swaps.append(rcopy(panel.at[:, :, pl.ds(away, BS)], SB.at[k], sib_s.at[k], sib_r.at[k], sibling))
        go(swaps[k])

    blocks = iota((16, 192), 1)
    member = jnp.zeros((16, 192), jnp.int32)
    named = lists[...]
    for m in range(160):
        member = jnp.where(named[:, m:m + 1] == blocks, 1, member)
    member = member.astype(F32).astype(BF16)
    pick_col = (iota((32, 192), 1) == 8 * iota((32, 192), 0) + col).astype(F32).astype(BF16)
    pick_row = (iota((8, 192), 1) == 32 * iota((8, 192), 0) + row).astype(F32).astype(BF16)
    in_col = lax.dot_general(pick_col, member, NT, preferred_element_type=F32).astype(BF16)
    in_row = lax.dot_general(pick_row, member, NT, preferred_element_type=F32).astype(BF16)
    for t in range(8):
        spread = ((iota((16, BS), 1) // 64 + 2 * t) == iota((16, BS), 0)).astype(F32).astype(BF16)
        MC[t] = jnp.dot(in_col, spread, preferred_element_type=F32)
    spread = ((iota((16, BS), 1) // 64 + 2 * col) == iota((16, BS), 0)).astype(F32).astype(BF16)
    RM[...] = jnp.dot(in_row, spread, preferred_element_type=F32)
    stored = pat[...].astype(F32).astype(BF16)
    stored = jnp.dot(pick_row, stored, preferred_element_type=F32).astype(BF16)
    stored = lax.dot_general(stored, pick_col, NT, preferred_element_type=F32).astype(BF16)
    for j in range(CBL):
        widen = (iota((32, BS), 0) == j).astype(F32).astype(BF16)
        PM[j] = jnp.dot(stored, widen, preferred_element_type=F32)

    def piece(k, xx, hh):
        return G.at[2 * k + c, :, :, pl.ds(pl.multiple_of((xx * 4 + hh) * 8, 8), 8), :]

    def wait_piece(k, xx, hh):
        ref = piece(k, xx, hh)
        rcopy(ref, ref, zs.at[0, 0], R.at[k, xx, hh], sibling).wait_recv()

    def send_piece(k, xx, hh, send, device):
        ref = piece(k, xx, hh)
        go(rcopy(ref, ref, send, R.at[k, xx, hh], device))

    def send_z(k):
        send_piece(k, x, h, zs.at[k, 0], dev(hh=(h + 1) % 4))
        send_piece(k, x, h, zs.at[k, 1], dev(hh=(h + 3) % 4))

    def send_x(k, d):
        hh = (h + d) % 4
        send_piece(k, x, hh, xs.at[k, d, 0], dev(xx=xp))
        send_piece(k, x, hh, xs.at[k, d, 1], dev(xx=xm))

    def group(tile, xx):
        return G.at[tile, :, :, pl.ds(pl.multiple_of(xx * 32, 32), 32), :]

    def send_group(k, xx):
        ref = group(2 * k + c, xx)
        go(rcopy(ref, ref, fs.at[k, xx], fr.at[k, xx], sibling))

    def assemble(k):
        t = 2 * k + c
        swaps[k].wait_recv()
        mine = panel[:, :, pl.ds(pl.multiple_of(t * BS, BS), BS)]
        other = SB[k]
        first = jnp.where(c == 0, mine, other)
        second = jnp.where(c == 0, other, mine)
        whole = jnp.concatenate([first, second], axis=1) * MC[t][:CBL][:, None, :]
        G[t, :, :, pl.ds(pl.multiple_of((x * 4 + h) * 8, 8), 8), :] = whole.reshape(6, 4, 8, BS)

    def stage_z(k):
        for d in (3, 1):
            hh = (h + d) % 4
            wait_piece(k, x, hh)
            if (d == 3) == (k % 2 == 0):
                send_piece(k, x, hh, zs.at[k, 2], dev(hh=(h + 4 - d) % 4))
            send_x(k, d)
        wait_piece(k, x, (h + 2) % 4)
        send_x(k, 2)
        send_group(k, x)

    def stage_x(k, fillers):
        for n, d in enumerate((0, 3, 1, 2)):
            hh = (h + d) % 4
            wait_piece(k, xm, hh)
            wait_piece(k, xp, hh)
            even = hh % 2 == 0
            send_piece(k, jnp.where(even, xm, xp), hh, xf.at[k, d], dev(xx=jnp.where(even, xp, xm)))
            fillers[n]()
        send_group(k, xm)
        send_group(k, xp)
        for d in (0, 3, 1, 2):
            wait_piece(k, x2, (h + d) % 4)
        send_group(k, x2)

    def prepare(a):
        loads[a].wait()

        def body(j, _):
            high, low = split(S32[a, j] * PM[j][a:a + 1, :])
            i, at = j // 6, pl.multiple_of((j % 6) * BS, BS)
            Shi[i, pl.ds(a * BS, BS), pl.ds(at, BS)] = high
            Slo[i, pl.ds(a * BS, BS), pl.ds(at, BS)] = low
            return 0

        lax.fori_loop(0, CBL, body, 0)

    def wait_groups(k):
        for xx in range(4):
            ref = group(2 * k + 1 - c, xx)
            rcopy(ref, ref, fs.at[0, 0], fr.at[k, xx], sibling).wait_recv()

    def multiply(k, i):
        for n in range(6):
            j = 6 * i + n
            for u in range(2):
                high, low = split(G[2 * k + u, j // 4, j % 4])
                Lhi[n * BS:(n + 1) * BS, u * BS:(u + 1) * BS] = high
                Llo[n * BS:(n + 1) * BS, u * BS:(u + 1) * BS] = low
        for b in range(2):
            rows = slice(384 * b, 384 * b + 384)
            total = jnp.dot(Shi[i, rows], Lhi[...], preferred_element_type=F32)
            total += jnp.dot(Shi[i, rows], Llo[...], preferred_element_type=F32)
            total += jnp.dot(Slo[i, rows], Lhi[...], preferred_element_type=F32)
            for u in range(2):
                part = total[:, u * BS:(u + 1) * BS]
                if i == 0:
                    O[k, u, rows] = part
                else:
                    O[k, u, rows] += part

    is_root = jnp.logical_and(y == h, zl == c)

    def mirror_copy(k, u):
        return rcopy(G.at[2 * k + u, :, x], MIR, ms.at[k, u], mr, (row, 2 * k + u))

    def mirror(k):
        for u in range(2):
            mine = col == 2 * k + u

            @pl.when(jnp.logical_and(is_root, jnp.logical_not(mine)))
            def _():
                mirror_copy(k, u).start()

            @pl.when(jnp.logical_and(is_root, mine))
            def _():
                MIR[...] = G[2 * k + u, :, x]

    def rows_of(yy):
        return pl.ds(pl.multiple_of(yy * SLICE, SLICE), SLICE)

    def scatter_y(k):
        for d in (2, 1, 3):
            yy = (y + d) % 4
            go(rcopy(O.at[k, :, rows_of(yy)], YR.at[k, y], ys.at[k, d - 1], yr.at[k, y], dev(yy=yy)))

    def finish_y(k):
        total = O[k, :, rows_of(y)]
        for d in (1, 3, 2):
            yy = (y + d) % 4
            rcopy(YR.at[k, yy], YR.at[k, yy], ys.at[0, 0], yr.at[k, yy], sibling).wait_recv()
            total += YR[k, yy]
        T[k] = total
        go(rcopy(T.at[k, 1 - zl], ZR.at[k], ws.at[k], wr.at[k], dev(zz=1 - zl)))

    def gather_copy(k):
        return rcopy(FB.at[k], XB.at[rows_of(y)], gs.at[k], gr.at[y], dev(yy=k))

    def finish_z(k):
        rcopy(ZR.at[k], ZR.at[k], ws.at[0], wr.at[k], sibling).wait_recv()
        total = T[k, zl] + ZR[k]

        @pl.when(y == k)
        def _():
            XB[rows_of(y)] = total

        @pl.when(y != k)
        def _():
            FB[k] = total
            gather_copy(k).start()

    def nothing():
        pass

    for k in range(NCHUNK):
        assemble(k)
        if k == 0:
            send_z(0)
            send_x(0, 0)
        if k == 1:
            send_z(1)
    prepare(0)
    prepare(1)
    stage_z(0)
    send_z(2)
    send_x(1, 0)
    prepare(2)
    prepare(3)
    stage_z(1)
    stage_x(0, [lambda: prepare(4), lambda: prepare(5), nothing, nothing])
    for k in range(1, NCHUNK):
        if k + 2 < NCHUNK:
            send_z(k + 2)
        if k + 1 < NCHUNK:
            send_x(k + 1, 0)
            stage_z(k + 1)
        wait_groups(k - 1)
        mirror(k - 1)
        stage_x(k, [lambda i=i: multiply(k - 1, i) for i in range(4)])
        scatter_y(k - 1)
        if k >= 2:
            finish_y(k - 2)
        if k >= 3:
            finish_z(k - 3)
    last = NCHUNK - 1
    wait_groups(last)
    mirror(last)
    for i in range(4):
        multiply(last, i)
    scatter_y(last)
    finish_y(last - 1)
    finish_z(last - 2)
    finish_y(last)
    finish_z(last - 1)
    finish_z(last)

    @pl.when(jnp.logical_not(is_root))
    def _():
        rcopy(MIR, MIR, ms.at[0, 0], mr, sibling).wait_recv()

    for d in (1, 3, 2):
        yy = (y + d) % 4
        rcopy(XB.at[rows_of(yy)], XB.at[rows_of(yy)], gs.at[0], gr.at[yy], sibling).wait_recv()
    full = jnp.zeros((BS, BS), F32)
    for a in range(RBL):
        value = -XB[a * BS:(a + 1) * BS] * RM[a:a + 1, :]
        solved[a, 0] = value
        vhi, vlo = split(value)
        mhi, mlo = split(MIR[a])
        full += lax.dot_general(mhi, vhi, TN, preferred_element_type=F32)
        full += lax.dot_general(mhi, vlo, TN, preferred_element_type=F32)
        full += lax.dot_general(mlo, vhi, TN, preferred_element_type=F32)
    packed = jnp.where(iota((64, BS), 1) < 64, full[:64], full[64:])

    DA[0] = packed
    copy = rcopy(DA.at[0], DA.at[1], ds_s.at[0], ds_r.at[0], sibling)
    go(copy)
    copy.wait_recv()
    DX[x] = DA[0] + DA[1]
    for d in (1, 2, 3):
        go(rcopy(DX.at[x], DX.at[x], ds_s.at[d], ds_r.at[1 + x], dev(xx=(x + d) % 4)))
    for d in (1, 2, 3):
        xx = (x + d) % 4
        rcopy(DX.at[xx], DX.at[xx], ds_s.at[0], ds_r.at[1 + xx], sibling).wait_recv()
    DH[h] = DX[0] + DX[1] + DX[2] + DX[3]
    for d in (1, 2, 3):
        go(rcopy(DH.at[h], DH.at[h], ds_s.at[3 + d], ds_r.at[5 + h], dev(hh=(h + d) % 4)))
    for d in (1, 2, 3):
        hh = (h + d) % 4
        rcopy(DH.at[hh], DH.at[hh], ds_s.at[0], ds_r.at[5 + hh], sibling).wait_recv()
    total = DH[0] + DH[1] + DH[2] + DH[3]
    diag_out[0] = diag[0] - total[:, :64]
    diag_out[1] = diag[1] - total[:, 64:]

    for copy in sends:
        copy.wait_send()
    for k in range(NCHUNK):
        @pl.when(y != k)
        def _():
            gather_copy(k).wait_send()

        for u in range(2):
            @pl.when(jnp.logical_and(is_root, col != 2 * k + u))
            def _():
                mirror_copy(k, u).wait_send()


def local(ancestor_inverse, block_pattern, ancestor_lists, panel, diag_term):
    vmem = pl.BlockSpec(memory_space=pltpu.VMEM)
    dma = pltpu.SemaphoreType.DMA
    return pl.pallas_call(
        kernel,
        out_shape=(jax.ShapeDtypeStruct((RBL, 1, BS, BS), F32), jax.ShapeDtypeStruct((2, 64, 64), F32)),
        in_specs=[vmem, pl.BlockSpec(memory_space=pl.ANY), vmem, vmem, vmem],
        out_specs=(vmem, vmem),
        scratch_shapes=[
            pltpu.VMEM((8, 6, 4, BS, BS), F32),
            pltpu.VMEM((NCHUNK, CBL, 4, BS), F32),
            pltpu.VMEM((RBL, CBL, BS, BS), F32),
            pltpu.VMEM((4, RBL * BS, 6 * BS), BF16),
            pltpu.VMEM((4, RBL * BS, 6 * BS), BF16),
            pltpu.VMEM((6 * BS, 2 * BS), BF16),
            pltpu.VMEM((6 * BS, 2 * BS), BF16),
            pltpu.VMEM((NCHUNK, 2, RBL * BS, BS), F32),
            pltpu.VMEM((NCHUNK, NY, 2, SLICE, BS), F32),
            pltpu.VMEM((NCHUNK, 2, SLICE, BS), F32),
            pltpu.VMEM((NCHUNK, SLICE, BS), F32),
            pltpu.VMEM((NCHUNK, SLICE, BS), F32),
            pltpu.VMEM((RBL * BS, BS), F32),
            pltpu.VMEM((RBL, BS, BS), F32),
            pltpu.VMEM((8, 32, BS), F32),
            pltpu.VMEM((8, BS), F32),
            pltpu.VMEM((CBL, 8, BS), F32),
            pltpu.VMEM((2, 64, BS), F32),
            pltpu.VMEM((NX, 64, BS), F32),
            pltpu.VMEM((NH, 64, BS), F32),
            dma((RBL,)),
            dma((NCHUNK,)), dma((NCHUNK,)),
            dma((NCHUNK, NX, NH)),
            dma((NCHUNK, 3)),
            dma((NCHUNK, NH, 2)),
            dma((NCHUNK, NH)),
            dma((NCHUNK, NX)), dma((NCHUNK, NX)),
            dma((NCHUNK, 3)), dma((NCHUNK, NY)),
            dma((NCHUNK,)), dma((NCHUNK,)),
            dma((NCHUNK,)), dma((NY,)),
            dma((NCHUNK, 2)), dma,
            dma((7,)), dma((9,)),
        ],
        compiler_params=pltpu.CompilerParams(collective_id=0, has_side_effects=True,
                                             vmem_limit_bytes=56 * 1024 * 1024),
    )(panel[:, 0], ancestor_inverse, block_pattern, ancestor_lists, diag_term)


def solution(mesh):
    placed = (
        P(None, "row", None, "col", None, None),
        P(),
        P(),
        P(None, "col", "row", None),
        P("col", None, None),
    )
    return jax.shard_map(
        local,
        mesh=mesh,
        in_specs=placed,
        out_specs=(P(None, "row", None, "col"), P("col", None, None)),
        check_vma=False,
    )
```

```python
import jax
import jax.numpy as jnp
from jax import lax
from jax.experimental import pallas as pl
from jax.experimental.pallas import tpu as pltpu
from jax.sharding import PartitionSpec as P

NX, NH, NC, NY, NZ = 4, 4, 2, 4, 2
NCHUNK = 4
RBL, CBL, BS = 6, 24, 128
SLICE = RBL * BS // NY
F32, BF16 = jnp.float32, jnp.bfloat16
NT = (((1,), (1,)), ((), ()))
TN = (((0,), (0,)), ((), ()))


def split(value):
    high = value.astype(BF16)
    return high, (value - high.astype(F32)).astype(BF16)


def iota(shape, dim):
    return lax.broadcasted_iota(jnp.int32, shape, dim)


def kernel(panel, s_hbm, pat, lists, diag, solved, diag_out,
           G, SB, S32, Shi, Slo, Lhi, Llo, O, YR, T, ZR, FB, XB, MIR, MC, RM, PM, DP, DA, DX, DH, DT,
           s_sem, sib_s, sib_r, R, zs, xs, xf, fs, fr, ys, yr, ws, wr, gs, gr, ms, mr, ds_s, ds_r):
    row, col = lax.axis_index("row"), lax.axis_index("col")
    x, h, c = row // 8, (row // 2) % 4, row % 2
    y, zl = col // 2, col % 2

    def dev(xx=x, hh=h, cc=c, yy=y, zz=zl):
        return (xx * 8 + hh * 2 + cc, yy * 2 + zz)

    def rcopy(src, dst, send, recv, device):
        return pltpu.make_async_remote_copy(src_ref=src, dst_ref=dst, send_sem=send, recv_sem=recv,
                                            device_id=device, device_id_type=pl.DeviceIdType.MESH)

    sibling = dev(cc=1 - c)
    xp, xm, x2 = (x + 1) % 4, (x + 3) % 4, (x + 2) % 4
    barrier = pltpu.get_barrier_semaphore()
    partners = [sibling]
    partners += [dev(xx=(x + d) % 4) for d in (1, 2, 3)]
    partners += [dev(hh=(h + d) % 4) for d in (1, 2, 3)]
    partners += [(row, (col + d) % 8) for d in range(1, 8)]
    for partner in partners:
        pl.semaphore_signal(barrier, inc=1, device_id=partner, device_id_type=pl.DeviceIdType.MESH)

    loads = [pltpu.make_async_copy(s_hbm.at[a, 0, :, 0], S32.at[a], s_sem.at[a]) for a in range(RBL)]
    for load in loads:
        load.start()
    blocks = iota((16, 192), 1)
    member = jnp.zeros((16, 192), jnp.int32)
    named = lists[...]
    for m in range(160):
        member = jnp.where(named[:, m:m + 1] == blocks, 1, member)
    member = member.astype(F32).astype(BF16)
    pick_col = (iota((32, 192), 1) == 8 * iota((32, 192), 0) + col).astype(F32).astype(BF16)
    pick_row = (iota((8, 192), 1) == 32 * iota((8, 192), 0) + row).astype(F32).astype(BF16)
    in_col = lax.dot_general(pick_col, member, NT, preferred_element_type=F32).astype(BF16)
    in_row = lax.dot_general(pick_row, member, NT, preferred_element_type=F32).astype(BF16)
    for t in range(8):
        spread = ((iota((16, BS), 1) // 64 + 2 * t) == iota((16, BS), 0)).astype(F32).astype(BF16)
        MC[t] = jnp.dot(in_col, spread, preferred_element_type=F32)
    spread = ((iota((16, BS), 1) // 64 + 2 * col) == iota((16, BS), 0)).astype(F32).astype(BF16)
    RM[...] = jnp.dot(in_row, spread, preferred_element_type=F32)
    stored = pat[...].astype(F32).astype(BF16)
    stored = jnp.dot(pick_row, stored, preferred_element_type=F32).astype(BF16)
    stored = lax.dot_general(stored, pick_col, NT, preferred_element_type=F32).astype(BF16)
    for j in range(CBL):
        widen = (iota((32, BS), 0) == j).astype(F32).astype(BF16)
        PM[j] = jnp.dot(stored, widen, preferred_element_type=F32)

    pl.semaphore_wait(barrier, len(partners))

    sends = []

    def go(copy):
        copy.start()
        sends.append(copy)

    swaps = []
    for k in range(NCHUNK):
        away = pl.multiple_of((2 * k + 1 - c) * BS, BS)
        swaps.append(rcopy(panel.at[:, :, pl.ds(away, BS)], SB.at[k], sib_s.at[k], sib_r.at[k], sibling))
        go(swaps[k])

    def piece(k, xx, hh):
        return G.at[2 * k + c, :, :, pl.ds(pl.multiple_of((xx * 4 + hh) * 8, 8), 8), :]

    def wait_piece(k, xx, hh):
        ref = piece(k, xx, hh)
        rcopy(ref, ref, zs.at[0, 0], R.at[k, xx, hh], sibling).wait_recv()

    def send_piece(k, xx, hh, send, device):
        ref = piece(k, xx, hh)
        go(rcopy(ref, ref, send, R.at[k, xx, hh], device))

    def send_z(k):
        send_piece(k, x, h, zs.at[k, 0], dev(hh=(h + 1) % 4))
        send_piece(k, x, h, zs.at[k, 1], dev(hh=(h + 3) % 4))
        send_piece(k, x, h, zs.at[k, 2], dev(hh=(h + 2) % 4))

    def send_x(k, d):
        hh = (h + d) % 4
        send_piece(k, x, hh, xs.at[k, d, 0], dev(xx=xp))
        send_piece(k, x, hh, xs.at[k, d, 1], dev(xx=xm))

    def group(tile, xx):
        return G.at[tile, :, :, pl.ds(pl.multiple_of(xx * 32, 32), 32), :]

    def send_group(k, xx):
        ref = group(2 * k + c, xx)
        go(rcopy(ref, ref, fs.at[k, xx], fr.at[k, xx], sibling))

    def assemble(k):
        t = 2 * k + c
        swaps[k].wait_recv()
        mine = panel[:, :, pl.ds(pl.multiple_of(t * BS, BS), BS)]
        other = SB[k]
        first = jnp.where(c == 0, mine, other)
        second = jnp.where(c == 0, other, mine)
        whole = jnp.concatenate([first, second], axis=1) * MC[t][:CBL][:, None, :]
        G[t, :, :, pl.ds(pl.multiple_of((x * 4 + h) * 8, 8), 8), :] = whole.reshape(6, 4, 8, BS)

    def stage_z(k):
        for d in (3, 1):
            hh = (h + d) % 4
            wait_piece(k, x, hh)
            send_x(k, d)
        wait_piece(k, x, (h + 2) % 4)
        send_x(k, 2)
        send_group(k, x)

    def stage_x(k, fillers):
        for n, d in enumerate((0, 3, 1, 2)):
            hh = (h + d) % 4
            wait_piece(k, xm, hh)
            wait_piece(k, xp, hh)
            even = hh % 2 == 0
            send_piece(k, jnp.where(even, xm, xp), hh, xf.at[k, d], dev(xx=jnp.where(even, xp, xm)))
            fillers[n]()
        send_group(k, xm)
        send_group(k, xp)

    def stage_far(k):
        for d in (0, 3, 1, 2):
            wait_piece(k, x2, (h + d) % 4)
        send_group(k, x2)

    lane = iota((BS, BS), 1)
    low_half, low_quarter = lane < 64, lane % 64 < 32

    def swap_lanes(mask, width, first, second):
        return (jnp.where(mask, first, pltpu.roll(second, width, 1)),
                jnp.where(mask, pltpu.roll(first, BS - width, 1), second))

    def prepare(a):
        loads[a].wait()

        def body(m, _):
            v = [S32[a, 4 * m + n] * PM[4 * m + n][a:a + 1, :] for n in range(4)]
            v[0], v[2] = swap_lanes(low_half, 64, v[0], v[2])
            v[1], v[3] = swap_lanes(low_half, 64, v[1], v[3])
            v[0], v[1] = swap_lanes(low_quarter, 32, v[0], v[1])
            v[2], v[3] = swap_lanes(low_quarter, 32, v[2], v[3])
            at = pl.multiple_of(m * BS, BS)
            for xx in range(4):
                high, low = split(v[xx])
                Shi[xx, pl.ds(a * BS, BS), pl.ds(at, BS)] = high
                Slo[xx, pl.ds(a * BS, BS), pl.ds(at, BS)] = low
            return 0

        lax.fori_loop(0, 6, body, 0)

    groups = (x, xm, xp, x2)

    def multiply(k, g):
        xx = groups[g]
        ref = group(2 * k + 1 - c, xx)
        rcopy(ref, ref, fs.at[0, 0], fr.at[k, xx], sibling).wait_recv()
        mirror(k, xx)
        for u in range(2):
            part = G[2 * k + u, :, :, pl.ds(pl.multiple_of(xx * 32, 32), 32), :].reshape(6 * BS, BS)
            high, low = split(part)
            Lhi[:, u * BS:(u + 1) * BS] = high
            Llo[:, u * BS:(u + 1) * BS] = low
        for b in range(2):
            rows = slice(384 * b, 384 * b + 384)
            total = jnp.dot(Shi[xx, rows], Lhi[...], preferred_element_type=F32)
            total += jnp.dot(Shi[xx, rows], Llo[...], preferred_element_type=F32)
            total += jnp.dot(Slo[xx, rows], Lhi[...], preferred_element_type=F32)
            for u in range(2):
                part = total[:, u * BS:(u + 1) * BS]
                if g == 0:
                    O[k, u, rows] = part
                else:
                    O[k, u, rows] += part

    is_root = jnp.logical_and(y == h, zl == c)

    def mirror_rows(xx):
        return pl.ds(pl.multiple_of(xx * 32, 32), 32)

    def mirror_copy(k, u, xx):
        return rcopy(G.at[2 * k + u, :, x, mirror_rows(xx)], MIR.at[:, mirror_rows(xx)], ms.at[k, u, xx], mr.at[xx],
                     (row, 2 * k + u))

    def mirror(k, xx):
        for u in range(2):
            mine = col == 2 * k + u

            @pl.when(jnp.logical_and(is_root, jnp.logical_not(mine)))
            def _():
                mirror_copy(k, u, xx).start()

            @pl.when(jnp.logical_and(is_root, mine))
            def _():
                MIR[:, mirror_rows(xx)] = G[2 * k + u, :, x, mirror_rows(xx)]

    def rows_of(yy):
        return pl.ds(pl.multiple_of(yy * SLICE, SLICE), SLICE)

    def scatter_y(k):
        for d in (2, 1, 3):
            yy = (y + d) % 4
            go(rcopy(O.at[k, :, rows_of(yy)], YR.at[k, y], ys.at[k, d - 1], yr.at[k, y], dev(yy=yy)))

    def finish_y(k):
        total = O[k, :, rows_of(y)]
        for d in (1, 3, 2):
            yy = (y + d) % 4
            rcopy(YR.at[k, yy], YR.at[k, yy], ys.at[0, 0], yr.at[k, yy], sibling).wait_recv()
            total += YR[k, yy]
        T[k] = total
        go(rcopy(T.at[k, 1 - zl], ZR.at[k], ws.at[k], wr.at[k], dev(zz=1 - zl)))

    def gather_copy(k):
        return rcopy(FB.at[k], XB.at[rows_of(y)], gs.at[k], gr.at[y], dev(yy=k))

    def finish_z(k):
        rcopy(ZR.at[k], ZR.at[k], ws.at[0], wr.at[k], sibling).wait_recv()
        total = T[k, zl] + ZR[k]

        @pl.when(y == k)
        def _():
            XB[rows_of(y)] = total

        @pl.when(y != k)
        def _():
            FB[k] = total
            gather_copy(k).start()

    def nothing():
        pass

    def fill(k):
        return [lambda g=g: multiply(k, g) for g in range(4)]

    prepare(0)
    for k in range(NCHUNK):
        assemble(k)
        if k < 2:
            send_z(k)
            send_x(k, 0)
    prepare(1)
    stage_z(0)
    send_z(2)
    send_x(2, 0)
    prepare(2)
    stage_z(1)
    stage_x(0, [lambda a=a: prepare(a) for a in (3, 4, 5)] + [nothing])
    send_z(3)
    send_x(3, 0)
    stage_z(2)
    stage_far(0)
    stage_x(1, fill(0))
    scatter_y(0)
    stage_z(3)
    stage_far(1)
    stage_x(2, fill(1))
    scatter_y(1)
    finish_y(0)
    stage_far(2)
    stage_x(3, fill(2))
    scatter_y(2)
    finish_y(1)
    finish_z(0)
    multiply(3, 0)
    multiply(3, 1)
    multiply(3, 2)
    stage_far(3)
    multiply(3, 3)
    scatter_y(3)
    finish_z(1)
    finish_y(2)
    finish_y(3)
    finish_z(2)
    finish_z(3)

    @pl.when(jnp.logical_not(is_root))
    def _():
        for xx in range(4):
            ref = MIR.at[:, mirror_rows(xx)]
            rcopy(ref, ref, ms.at[0, 0, 0], mr.at[xx], sibling).wait_recv()

    for d in (1, 3, 2):
        yy = (y + d) % 4
        rcopy(XB.at[rows_of(yy)], XB.at[rows_of(yy)], gs.at[0], gr.at[yy], sibling).wait_recv()
    full = jnp.zeros((BS, BS), F32)
    for a in range(RBL):
        value = -XB[a * BS:(a + 1) * BS] * RM[a:a + 1, :]
        solved[a, 0] = value
        vhi, vlo = split(value)
        mhi, mlo = split(MIR[a])
        full += lax.dot_general(mhi, vhi, TN, preferred_element_type=F32)
        full += lax.dot_general(mhi, vlo, TN, preferred_element_type=F32)
        full += lax.dot_general(mlo, vhi, TN, preferred_element_type=F32)
    packed = jnp.where(iota((64, BS), 1) < 64, full[:64], full[64:])

    def half(cc):
        return pl.ds(pl.multiple_of(cc * 32, 32), 32)

    DP[...] = packed
    copy = rcopy(DP.at[half(1 - c)], DA, ds_s.at[0], ds_r.at[0], sibling)
    go(copy)
    copy.wait_recv()
    DX[x] = DP[half(c)] + DA[...]
    for d in (2, 1, 3):
        go(rcopy(DX.at[x], DX.at[x], ds_s.at[d], ds_r.at[1 + x], dev(xx=(x + d) % 4)))
    for d in (1, 2, 3):
        xx = (x + d) % 4
        rcopy(DX.at[xx], DX.at[xx], ds_s.at[0], ds_r.at[1 + xx], sibling).wait_recv()
    DH[h] = DX[0] + DX[1] + DX[2] + DX[3]
    for d in (2, 1, 3):
        go(rcopy(DH.at[h], DH.at[h], ds_s.at[3 + d], ds_r.at[5 + h], dev(hh=(h + d) % 4)))
    for d in (1, 2, 3):
        hh = (h + d) % 4
        rcopy(DH.at[hh], DH.at[hh], ds_s.at[0], ds_r.at[5 + hh], sibling).wait_recv()
    DT[half(c)] = DH[0] + DH[1] + DH[2] + DH[3]
    go(rcopy(DT.at[half(c)], DT.at[half(c)], ds_s.at[7], ds_r.at[9], sibling))
    other = DT.at[half(1 - c)]
    rcopy(other, other, ds_s.at[0], ds_r.at[9], sibling).wait_recv()
    total = DT[...]
    diag_out[0] = diag[0] - total[:, :64]
    diag_out[1] = diag[1] - total[:, 64:]

    for copy in sends:
        copy.wait_send()
    for k in range(NCHUNK):
        @pl.when(y != k)
        def _():
            gather_copy(k).wait_send()

        for u in range(2):
            @pl.when(jnp.logical_and(is_root, col != 2 * k + u))
            def _():
                for xx in range(4):
                    mirror_copy(k, u, xx).wait_send()


def local(ancestor_inverse, block_pattern, ancestor_lists, panel, diag_term):
    vmem = pl.BlockSpec(memory_space=pltpu.VMEM)
    dma = pltpu.SemaphoreType.DMA
    return pl.pallas_call(
        kernel,
        out_shape=(jax.ShapeDtypeStruct((RBL, 1, BS, BS), F32), jax.ShapeDtypeStruct((2, 64, 64), F32)),
        in_specs=[vmem, pl.BlockSpec(memory_space=pl.ANY), vmem, vmem, vmem],
        out_specs=(vmem, vmem),
        scratch_shapes=[
            pltpu.VMEM((8, 6, 4, BS, BS), F32),
            pltpu.VMEM((NCHUNK, CBL, 4, BS), F32),
            pltpu.VMEM((RBL, CBL, BS, BS), F32),
            pltpu.VMEM((4, RBL * BS, 6 * BS), BF16),
            pltpu.VMEM((4, RBL * BS, 6 * BS), BF16),
            pltpu.VMEM((6 * BS, 2 * BS), BF16),
            pltpu.VMEM((6 * BS, 2 * BS), BF16),
            pltpu.VMEM((NCHUNK, 2, RBL * BS, BS), F32),
            pltpu.VMEM((NCHUNK, NY, 2, SLICE, BS), F32),
            pltpu.VMEM((NCHUNK, 2, SLICE, BS), F32),
            pltpu.VMEM((NCHUNK, SLICE, BS), F32),
            pltpu.VMEM((NCHUNK, SLICE, BS), F32),
            pltpu.VMEM((RBL * BS, BS), F32),
            pltpu.VMEM((RBL, BS, BS), F32),
            pltpu.VMEM((8, 32, BS), F32),
            pltpu.VMEM((8, BS), F32),
            pltpu.VMEM((CBL, 8, BS), F32),
            pltpu.VMEM((64, BS), F32),
            pltpu.VMEM((32, BS), F32),
            pltpu.VMEM((NX, 32, BS), F32),
            pltpu.VMEM((NH, 32, BS), F32),
            pltpu.VMEM((64, BS), F32),
            dma((RBL,)),
            dma((NCHUNK,)), dma((NCHUNK,)),
            dma((NCHUNK, NX, NH)),
            dma((NCHUNK, 3)),
            dma((NCHUNK, NH, 2)),
            dma((NCHUNK, NH)),
            dma((NCHUNK, NX)), dma((NCHUNK, NX)),
            dma((NCHUNK, 3)), dma((NCHUNK, NY)),
            dma((NCHUNK,)), dma((NCHUNK,)),
            dma((NCHUNK,)), dma((NY,)),
            dma((NCHUNK, 2, 4)), dma((4,)),
            dma((8,)), dma((10,)),
        ],
        compiler_params=pltpu.CompilerParams(collective_id=0, has_side_effects=True,
                                             vmem_limit_bytes=56 * 1024 * 1024),
    )(panel[:, 0], ancestor_inverse, block_pattern, ancestor_lists, diag_term)


def solution(mesh):
    placed = (
        P(None, "row", None, "col", None, None),
        P(),
        P(),
        P(None, "col", "row", None),
        P("col", None, None),
    )
    return jax.shard_map(
        local,
        mesh=mesh,
        in_specs=placed,
        out_specs=(P(None, "row", None, "col"), P("col", None, None)),
        check_vma=False,
    )
```

```python
import jax
import jax.numpy as jnp
from jax import lax
from jax.experimental import pallas as pl
from jax.experimental.pallas import tpu as pltpu
from jax.sharding import PartitionSpec as P

NX, NH, NC, NY, NZ = 4, 4, 2, 4, 2
NCHUNK = 4
RBL, CBL, BS = 6, 24, 128
SLICE = RBL * BS // NY
F32, BF16 = jnp.float32, jnp.bfloat16
NT = (((1,), (1,)), ((), ()))
TN = (((0,), (0,)), ((), ()))


def split(value):
    high = value.astype(BF16)
    return high, (value - high.astype(F32)).astype(BF16)


def iota(shape, dim):
    return lax.broadcasted_iota(jnp.int32, shape, dim)


def kernel(panel, s_hbm, pat, lists, diag, solved, diag_out,
           G, SB, S32, Shi, Slo, Lhi, Llo, O, YR, T, ZR, FB, XB, MIR, MC, RM, PM, DP, DA, DX, DH,
           s_sem, sib_s, sib_r, R, zs, xs, xf, fs, fr, ys, yr, ws, wr, gs, gr, ms, mr, ds_s, ds_r):
    row, col = lax.axis_index("row"), lax.axis_index("col")
    x, h, c = row // 8, (row // 2) % 4, row % 2
    y, zl = col // 2, col % 2

    def dev(xx=x, hh=h, cc=c, yy=y, zz=zl):
        return (xx * 8 + hh * 2 + cc, yy * 2 + zz)

    def rcopy(src, dst, send, recv, device):
        return pltpu.make_async_remote_copy(src_ref=src, dst_ref=dst, send_sem=send, recv_sem=recv,
                                            device_id=device, device_id_type=pl.DeviceIdType.MESH)

    sibling = dev(cc=1 - c)
    xp, xm, x2 = (x + 1) % 4, (x + 3) % 4, (x + 2) % 4
    barrier = pltpu.get_barrier_semaphore()
    partners = [sibling]
    partners += [dev(xx=(x + d) % 4) for d in (1, 2, 3)]
    partners += [dev(hh=(h + d) % 4) for d in (1, 2, 3)]
    partners += [(row, (col + d) % 8) for d in range(1, 8)]
    for partner in partners:
        pl.semaphore_signal(barrier, inc=1, device_id=partner, device_id_type=pl.DeviceIdType.MESH)

    loads = [pltpu.make_async_copy(s_hbm.at[a, 0, :, 0], S32.at[a], s_sem.at[a]) for a in range(RBL)]
    for load in loads:
        load.start()
    blocks = iota((16, 192), 1)
    member = jnp.zeros((16, 192), jnp.int32)
    named = lists[...]
    for m in range(160):
        member = jnp.where(named[:, m:m + 1] == blocks, 1, member)
    member = member.astype(F32).astype(BF16)
    pick_col = (iota((32, 192), 1) == 8 * iota((32, 192), 0) + col).astype(F32).astype(BF16)
    pick_row = (iota((8, 192), 1) == 32 * iota((8, 192), 0) + row).astype(F32).astype(BF16)
    in_col = lax.dot_general(pick_col, member, NT, preferred_element_type=F32).astype(BF16)
    in_row = lax.dot_general(pick_row, member, NT, preferred_element_type=F32).astype(BF16)
    for t in range(8):
        spread = ((iota((16, BS), 1) // 64 + 2 * t) == iota((16, BS), 0)).astype(F32).astype(BF16)
        MC[t] = jnp.dot(in_col, spread, preferred_element_type=F32)
    spread = ((iota((16, BS), 1) // 64 + 2 * col) == iota((16, BS), 0)).astype(F32).astype(BF16)
    RM[...] = jnp.dot(in_row, spread, preferred_element_type=F32)
    stored = pat[...].astype(F32).astype(BF16)
    stored = jnp.dot(pick_row, stored, preferred_element_type=F32).astype(BF16)
    stored = lax.dot_general(stored, pick_col, NT, preferred_element_type=F32).astype(BF16)
    for j in range(CBL):
        widen = (iota((32, BS), 0) == j).astype(F32).astype(BF16)
        PM[j] = jnp.dot(stored, widen, preferred_element_type=F32)

    pl.semaphore_wait(barrier, len(partners))

    sends = []

    def go(copy):
        copy.start()
        sends.append(copy)

    swaps = []
    for k in range(NCHUNK):
        away = pl.multiple_of((2 * k + 1 - c) * BS, BS)
        swaps.append(rcopy(panel.at[:, :, pl.ds(away, BS)], SB.at[k], sib_s.at[k], sib_r.at[k], sibling))
        go(swaps[k])

    def piece(k, xx, hh):
        return G.at[2 * k + c, :, :, pl.ds(pl.multiple_of((xx * 4 + hh) * 8, 8), 8), :]

    def wait_piece(k, xx, hh):
        ref = piece(k, xx, hh)
        rcopy(ref, ref, zs.at[0, 0], R.at[k, xx, hh], sibling).wait_recv()

    def send_piece(k, xx, hh, send, device):
        ref = piece(k, xx, hh)
        go(rcopy(ref, ref, send, R.at[k, xx, hh], device))

    def send_z(k):
        send_piece(k, x, h, zs.at[k, 0], dev(hh=(h + 1) % 4))
        send_piece(k, x, h, zs.at[k, 1], dev(hh=(h + 3) % 4))
        send_piece(k, x, h, zs.at[k, 2], dev(hh=(h + 2) % 4))

    def send_x(k, d):
        hh = (h + d) % 4
        send_piece(k, x, hh, xs.at[k, d, 0], dev(xx=xp))
        send_piece(k, x, hh, xs.at[k, d, 1], dev(xx=xm))

    def group(tile, xx):
        return G.at[tile, :, :, pl.ds(pl.multiple_of(xx * 32, 32), 32), :]

    def send_group(k, xx):
        ref = group(2 * k + c, xx)
        go(rcopy(ref, ref, fs.at[k, xx], fr.at[k, xx], sibling))

    def assemble(k):
        t = 2 * k + c
        swaps[k].wait_recv()
        mine = panel[:, :, pl.ds(pl.multiple_of(t * BS, BS), BS)]
        other = SB[k]
        first = jnp.where(c == 0, mine, other)
        second = jnp.where(c == 0, other, mine)
        whole = jnp.concatenate([first, second], axis=1) * MC[t][:CBL][:, None, :]
        G[t, :, :, pl.ds(pl.multiple_of((x * 4 + h) * 8, 8), 8), :] = whole.reshape(6, 4, 8, BS)

    def stage_z(k):
        for d in (3, 1):
            hh = (h + d) % 4
            wait_piece(k, x, hh)
            send_x(k, d)
        wait_piece(k, x, (h + 2) % 4)
        send_x(k, 2)
        send_group(k, x)

    def stage_x(k, fillers):
        for n, d in enumerate((0, 3, 1, 2)):
            hh = (h + d) % 4
            wait_piece(k, xm, hh)
            wait_piece(k, xp, hh)
            even = hh % 2 == 0
            send_piece(k, jnp.where(even, xm, xp), hh, xf.at[k, d], dev(xx=jnp.where(even, xp, xm)))
            fillers[n]()
        send_group(k, xm)
        send_group(k, xp)

    def stage_far(k):
        for d in (0, 3, 1, 2):
            wait_piece(k, x2, (h + d) % 4)
        send_group(k, x2)

    lane = iota((BS, BS), 1)
    low_half, low_quarter = lane < 64, lane % 64 < 32

    def swap_lanes(mask, width, first, second):
        return (jnp.where(mask, first, pltpu.roll(second, width, 1)),
                jnp.where(mask, pltpu.roll(first, BS - width, 1), second))

    def prepare(a):
        loads[a].wait()

        def body(m, _):
            v = [S32[a, 4 * m + n] * PM[4 * m + n][a:a + 1, :] for n in range(4)]
            v[0], v[2] = swap_lanes(low_half, 64, v[0], v[2])
            v[1], v[3] = swap_lanes(low_half, 64, v[1], v[3])
            v[0], v[1] = swap_lanes(low_quarter, 32, v[0], v[1])
            v[2], v[3] = swap_lanes(low_quarter, 32, v[2], v[3])
            at = pl.multiple_of(m * BS, BS)
            for xx in range(4):
                high, low = split(v[xx])
                Shi[xx, pl.ds(a * BS, BS), pl.ds(at, BS)] = high
                Slo[xx, pl.ds(a * BS, BS), pl.ds(at, BS)] = low
            return 0

        lax.fori_loop(0, 6, body, 0)

    groups = (x, xm, xp, x2)

    def multiply(k, g):
        xx = groups[g]
        ref = group(2 * k + 1 - c, xx)
        rcopy(ref, ref, fs.at[0, 0], fr.at[k, xx], sibling).wait_recv()
        mirror(k, xx)
        for u in range(2):
            part = G[2 * k + u, :, :, pl.ds(pl.multiple_of(xx * 32, 32), 32), :].reshape(6 * BS, BS)
            high, low = split(part)
            Lhi[:, u * BS:(u + 1) * BS] = high
            Llo[:, u * BS:(u + 1) * BS] = low
        for b in range(2):
            rows = slice(384 * b, 384 * b + 384)
            total = jnp.dot(Shi[xx, rows], Lhi[...], preferred_element_type=F32)
            total += jnp.dot(Shi[xx, rows], Llo[...], preferred_element_type=F32)
            total += jnp.dot(Slo[xx, rows], Lhi[...], preferred_element_type=F32)
            for u in range(2):
                part = total[:, u * BS:(u + 1) * BS]
                if g == 0:
                    O[k, u, rows] = part
                else:
                    O[k, u, rows] += part

    is_root = jnp.logical_and(y == h, zl == c)

    def mirror_rows(xx):
        return pl.ds(pl.multiple_of(xx * 32, 32), 32)

    def mirror_copy(k, u, xx):
        return rcopy(G.at[2 * k + u, :, x, mirror_rows(xx)], MIR.at[:, mirror_rows(xx)], ms.at[k, u, xx], mr.at[xx],
                     (row, 2 * k + u))

    def mirror(k, xx):
        for u in range(2):
            mine = col == 2 * k + u

            @pl.when(jnp.logical_and(is_root, jnp.logical_not(mine)))
            def _():
                mirror_copy(k, u, xx).start()

            @pl.when(jnp.logical_and(is_root, mine))
            def _():
                MIR[:, mirror_rows(xx)] = G[2 * k + u, :, x, mirror_rows(xx)]

    def rows_of(yy):
        return pl.ds(pl.multiple_of(yy * SLICE, SLICE), SLICE)

    def scatter_y(k):
        for d in (2, 1, 3):
            yy = (y + d) % 4
            go(rcopy(O.at[k, :, rows_of(yy)], YR.at[k, y], ys.at[k, d - 1], yr.at[k, y], dev(yy=yy)))

    def finish_y(k):
        total = O[k, :, rows_of(y)]
        for d in (1, 3, 2):
            yy = (y + d) % 4
            rcopy(YR.at[k, yy], YR.at[k, yy], ys.at[0, 0], yr.at[k, yy], sibling).wait_recv()
            total += YR[k, yy]
        T[k] = total
        go(rcopy(T.at[k, 1 - zl], ZR.at[k], ws.at[k], wr.at[k], dev(zz=1 - zl)))

    def gather_copy(k):
        return rcopy(FB.at[k], XB.at[rows_of(y)], gs.at[k], gr.at[y], dev(yy=k))

    def finish_z(k):
        rcopy(ZR.at[k], ZR.at[k], ws.at[0], wr.at[k], sibling).wait_recv()
        total = T[k, zl] + ZR[k]

        @pl.when(y == k)
        def _():
            XB[rows_of(y)] = total

        @pl.when(y != k)
        def _():
            FB[k] = total
            gather_copy(k).start()

    def nothing():
        pass

    def fill(k):
        return [lambda g=g: multiply(k, g) for g in range(4)]

    for k in range(NCHUNK):
        assemble(k)
        if k < 2:
            send_z(k)
            send_x(k, 0)
    prepare(0)
    prepare(1)
    stage_z(0)
    send_z(2)
    send_x(2, 0)
    prepare(2)
    stage_z(1)
    stage_x(0, [lambda a=a: prepare(a) for a in (3, 4, 5)] + [nothing])
    send_z(3)
    send_x(3, 0)
    stage_z(2)
    stage_far(0)
    stage_x(1, fill(0))
    scatter_y(0)
    stage_z(3)
    stage_far(1)
    stage_x(2, fill(1))
    scatter_y(1)
    finish_y(0)
    stage_far(2)
    stage_x(3, fill(2))
    scatter_y(2)
    finish_y(1)
    finish_z(0)
    multiply(3, 0)
    multiply(3, 1)
    multiply(3, 2)
    stage_far(3)
    multiply(3, 3)
    scatter_y(3)
    finish_z(1)
    finish_y(2)
    finish_y(3)
    finish_z(2)
    finish_z(3)

    @pl.when(jnp.logical_not(is_root))
    def _():
        for xx in range(4):
            ref = MIR.at[:, mirror_rows(xx)]
            rcopy(ref, ref, ms.at[0, 0, 0], mr.at[xx], sibling).wait_recv()

    for d in (1, 3, 2):
        yy = (y + d) % 4
        rcopy(XB.at[rows_of(yy)], XB.at[rows_of(yy)], gs.at[0], gr.at[yy], sibling).wait_recv()
    full = jnp.zeros((BS, BS), F32)
    for a in range(RBL):
        value = -XB[a * BS:(a + 1) * BS] * RM[a:a + 1, :]
        solved[a, 0] = value
        vhi, vlo = split(value)
        mhi, mlo = split(MIR[a])
        full += lax.dot_general(mhi, vhi, TN, preferred_element_type=F32)
        full += lax.dot_general(mhi, vlo, TN, preferred_element_type=F32)
        full += lax.dot_general(mlo, vhi, TN, preferred_element_type=F32)
    packed = jnp.where(iota((64, BS), 1) < 64, full[:64], full[64:])

    DP[...] = packed
    copy = rcopy(DP, DA, ds_s.at[0], ds_r.at[0], sibling)
    go(copy)
    copy.wait_recv()
    DX[x] = DP[...] + DA[...]
    for d in (2, 1, 3):
        go(rcopy(DX.at[x], DX.at[x], ds_s.at[d], ds_r.at[1 + x], dev(xx=(x + d) % 4)))
    for d in (1, 2, 3):
        xx = (x + d) % 4
        rcopy(DX.at[xx], DX.at[xx], ds_s.at[0], ds_r.at[1 + xx], sibling).wait_recv()
    DH[h] = DX[0] + DX[1] + DX[2] + DX[3]
    for d in (2, 1, 3):
        go(rcopy(DH.at[h], DH.at[h], ds_s.at[3 + d], ds_r.at[5 + h], dev(hh=(h + d) % 4)))
    for d in (1, 2, 3):
        hh = (h + d) % 4
        rcopy(DH.at[hh], DH.at[hh], ds_s.at[0], ds_r.at[5 + hh], sibling).wait_recv()
    total = DH[0] + DH[1] + DH[2] + DH[3]
    diag_out[0] = diag[0] - total[:, :64]
    diag_out[1] = diag[1] - total[:, 64:]

    for copy in sends:
        copy.wait_send()
    for k in range(NCHUNK):
        @pl.when(y != k)
        def _():
            gather_copy(k).wait_send()

        for u in range(2):
            @pl.when(jnp.logical_and(is_root, col != 2 * k + u))
            def _():
                for xx in range(4):
                    mirror_copy(k, u, xx).wait_send()


def finish(rows, diag, rows_out, diag_out):
    rows_out[...] = rows[...]
    diag_out[...] = diag[...]


def local(ancestor_inverse, block_pattern, ancestor_lists, panel, diag_term):
    vmem = pl.BlockSpec(memory_space=pltpu.VMEM)
    dma = pltpu.SemaphoreType.DMA
    shapes = (jax.ShapeDtypeStruct((RBL, 1, BS, BS), F32), jax.ShapeDtypeStruct((2, 64, 64), F32))
    rows, diag = pl.pallas_call(
        kernel,
        out_shape=shapes,
        in_specs=[vmem, pl.BlockSpec(memory_space=pl.ANY), vmem, vmem, vmem],
        out_specs=(vmem, vmem),
        scratch_shapes=[
            pltpu.VMEM((8, 6, 4, BS, BS), F32),
            pltpu.VMEM((NCHUNK, CBL, 4, BS), F32),
            pltpu.VMEM((RBL, CBL, BS, BS), F32),
            pltpu.VMEM((4, RBL * BS, 6 * BS), BF16),
            pltpu.VMEM((4, RBL * BS, 6 * BS), BF16),
            pltpu.VMEM((6 * BS, 2 * BS), BF16),
            pltpu.VMEM((6 * BS, 2 * BS), BF16),
            pltpu.VMEM((NCHUNK, 2, RBL * BS, BS), F32),
            pltpu.VMEM((NCHUNK, NY, 2, SLICE, BS), F32),
            pltpu.VMEM((NCHUNK, 2, SLICE, BS), F32),
            pltpu.VMEM((NCHUNK, SLICE, BS), F32),
            pltpu.VMEM((NCHUNK, SLICE, BS), F32),
            pltpu.VMEM((RBL * BS, BS), F32),
            pltpu.VMEM((RBL, BS, BS), F32),
            pltpu.VMEM((8, 32, BS), F32),
            pltpu.VMEM((8, BS), F32),
            pltpu.VMEM((CBL, 8, BS), F32),
            pltpu.VMEM((64, BS), F32),
            pltpu.VMEM((64, BS), F32),
            pltpu.VMEM((NX, 64, BS), F32),
            pltpu.VMEM((NH, 64, BS), F32),
            dma((RBL,)),
            dma((NCHUNK,)), dma((NCHUNK,)),
            dma((NCHUNK, NX, NH)),
            dma((NCHUNK, 3)),
            dma((NCHUNK, NH, 2)),
            dma((NCHUNK, NH)),
            dma((NCHUNK, NX)), dma((NCHUNK, NX)),
            dma((NCHUNK, 3)), dma((NCHUNK, NY)),
            dma((NCHUNK,)), dma((NCHUNK,)),
            dma((NCHUNK,)), dma((NY,)),
            dma((NCHUNK, 2, 4)), dma((4,)),
            dma((8,)), dma((10,)),
        ],
        compiler_params=pltpu.CompilerParams(collective_id=0, has_side_effects=True,
                                             vmem_limit_bytes=56 * 1024 * 1024),
    )(panel[:, 0], ancestor_inverse, block_pattern, ancestor_lists, diag_term)
    return pl.pallas_call(finish, out_shape=shapes, in_specs=[vmem, vmem], out_specs=(vmem, vmem))(rows, diag)


def solution(mesh):
    placed = (
        P(None, "row", None, "col", None, None),
        P(),
        P(),
        P(None, "col", "row", None),
        P("col", None, None),
    )
    return jax.shard_map(
        local,
        mesh=mesh,
        in_specs=placed,
        out_specs=(P(None, "row", None, "col"), P("col", None, None)),
        check_vma=False,
    )
```

```python
import jax
import jax.numpy as jnp
from jax import lax
from jax.experimental import pallas as pl
from jax.experimental.pallas import tpu as pltpu
from jax.sharding import PartitionSpec as P

NX, NH, NC, NY, NZ = 4, 4, 2, 4, 2
NCHUNK = 4
RBL, CBL, BS = 6, 24, 128
SLICE = RBL * BS // NY
F32, BF16 = jnp.float32, jnp.bfloat16
NT = (((1,), (1,)), ((), ()))
TN = (((0,), (0,)), ((), ()))


def split(value):
    high = value.astype(BF16)
    return high, (value - high.astype(F32)).astype(BF16)


def iota(shape, dim):
    return lax.broadcasted_iota(jnp.int32, shape, dim)


def kernel(panel, s_hbm, pat, lists, diag, solved, diag_out,
           G, SB, S32, Shi, Slo, Lhi, Llo, O, YR, T, ZR, FB, XB, MIR, MC, RM, PM, DP, DA, DX, DH,
           s_sem, sib_s, sib_r, R, zs, xs, xf, fs, fr, ys, yr, ws, wr, gs, gr, ms, mr, ds_s, ds_r):
    row, col = lax.axis_index("row"), lax.axis_index("col")
    x, h, c = row // 8, (row // 2) % 4, row % 2
    y, zl = col // 2, col % 2

    def dev(xx=x, hh=h, cc=c, yy=y, zz=zl):
        return (xx * 8 + hh * 2 + cc, yy * 2 + zz)

    def rcopy(src, dst, send, recv, device):
        return pltpu.make_async_remote_copy(src_ref=src, dst_ref=dst, send_sem=send, recv_sem=recv,
                                            device_id=device, device_id_type=pl.DeviceIdType.MESH)

    sibling = dev(cc=1 - c)
    xp, xm, x2 = (x + 1) % 4, (x + 3) % 4, (x + 2) % 4
    barrier = pltpu.get_barrier_semaphore()
    partners = [sibling]
    partners += [dev(xx=(x + d) % 4) for d in (1, 2, 3)]
    partners += [dev(hh=(h + d) % 4) for d in (1, 2, 3)]
    partners += [(row, (col + d) % 8) for d in range(1, 8)]
    for partner in partners:
        pl.semaphore_signal(barrier, inc=1, device_id=partner, device_id_type=pl.DeviceIdType.MESH)

    loads = [pltpu.make_async_copy(s_hbm.at[a, 0, :, 0], S32.at[a], s_sem.at[a]) for a in range(RBL)]
    for load in loads:
        load.start()
    blocks = iota((16, 192), 1)
    member = jnp.zeros((16, 192), jnp.int32)
    named = lists[...]
    for m in range(160):
        member = jnp.where(named[:, m:m + 1] == blocks, 1, member)
    member = member.astype(F32).astype(BF16)
    pick_col = (iota((32, 192), 1) == 8 * iota((32, 192), 0) + col).astype(F32).astype(BF16)
    pick_row = (iota((8, 192), 1) == 32 * iota((8, 192), 0) + row).astype(F32).astype(BF16)
    in_col = lax.dot_general(pick_col, member, NT, preferred_element_type=F32).astype(BF16)
    in_row = lax.dot_general(pick_row, member, NT, preferred_element_type=F32).astype(BF16)
    for t in range(8):
        spread = ((iota((16, BS), 1) // 64 + 2 * t) == iota((16, BS), 0)).astype(F32).astype(BF16)
        MC[t] = jnp.dot(in_col, spread, preferred_element_type=F32)
    spread = ((iota((16, BS), 1) // 64 + 2 * col) == iota((16, BS), 0)).astype(F32).astype(BF16)
    RM[...] = jnp.dot(in_row, spread, preferred_element_type=F32)
    stored = pat[...].astype(F32).astype(BF16)
    stored = jnp.dot(pick_row, stored, preferred_element_type=F32).astype(BF16)
    stored = lax.dot_general(stored, pick_col, NT, preferred_element_type=F32).astype(BF16)
    for j in range(CBL):
        widen = (iota((32, BS), 0) == j).astype(F32).astype(BF16)
        PM[j] = jnp.dot(stored, widen, preferred_element_type=F32)

    pl.semaphore_wait(barrier, len(partners))

    sends = []

    def go(copy):
        copy.start()
        sends.append(copy)

    swaps = []
    for k in range(NCHUNK):
        away = pl.multiple_of((2 * k + 1 - c) * BS, BS)
        swaps.append(rcopy(panel.at[:, :, pl.ds(away, BS)], SB.at[k], sib_s.at[k], sib_r.at[k], sibling))
        go(swaps[k])

    def piece(k, xx, hh):
        return G.at[2 * k + c, :, :, pl.ds(pl.multiple_of((xx * 4 + hh) * 8, 8), 8), :]

    def wait_piece(k, xx, hh):
        ref = piece(k, xx, hh)
        rcopy(ref, ref, zs.at[0, 0], R.at[k, xx, hh], sibling).wait_recv()

    def send_piece(k, xx, hh, send, device):
        ref = piece(k, xx, hh)
        go(rcopy(ref, ref, send, R.at[k, xx, hh], device))

    def send_z(k):
        send_piece(k, x, h, zs.at[k, 0], dev(hh=(h + 1) % 4))
        send_piece(k, x, h, zs.at[k, 1], dev(hh=(h + 3) % 4))
        send_piece(k, x, h, zs.at[k, 2], dev(hh=(h + 2) % 4))

    def send_x(k, d):
        hh = (h + d) % 4
        send_piece(k, x, hh, xs.at[k, d, 0], dev(xx=xp))
        send_piece(k, x, hh, xs.at[k, d, 1], dev(xx=xm))

    def group(tile, xx):
        return G.at[tile, :, :, pl.ds(pl.multiple_of(xx * 32, 32), 32), :]

    def send_group(k, xx):
        ref = group(2 * k + c, xx)
        go(rcopy(ref, ref, fs.at[k, xx], fr.at[k, xx], sibling))

    def assemble(k):
        t = 2 * k + c
        swaps[k].wait_recv()
        mine = panel[:, :, pl.ds(pl.multiple_of(t * BS, BS), BS)]
        other = SB[k]
        first = jnp.where(c == 0, mine, other)
        second = jnp.where(c == 0, other, mine)
        whole = jnp.concatenate([first, second], axis=1) * MC[t][:CBL][:, None, :]
        G[t, :, :, pl.ds(pl.multiple_of((x * 4 + h) * 8, 8), 8), :] = whole.reshape(6, 4, 8, BS)

    def stage_z(k):
        for d in (3, 1):
            hh = (h + d) % 4
            wait_piece(k, x, hh)
            send_x(k, d)
        wait_piece(k, x, (h + 2) % 4)
        send_x(k, 2)
        send_group(k, x)

    def stage_x(k, fillers):
        for n, d in enumerate((0, 3, 1, 2)):
            hh = (h + d) % 4
            wait_piece(k, xm, hh)
            wait_piece(k, xp, hh)
            even = hh % 2 == 0
            send_piece(k, jnp.where(even, xm, xp), hh, xf.at[k, d], dev(xx=jnp.where(even, xp, xm)))
            if n >= 2:
                fillers[n - 2]()
        send_group(k, xm)
        send_group(k, xp)
        fillers[2]()
        fillers[3]()

    def stage_far(k):
        for d in (0, 3, 1, 2):
            wait_piece(k, x2, (h + d) % 4)
        send_group(k, x2)

    lane = iota((BS, BS), 1)
    low_half, low_quarter = lane < 64, lane % 64 < 32

    def swap_lanes(mask, width, first, second):
        return (jnp.where(mask, first, pltpu.roll(second, width, 1)),
                jnp.where(mask, pltpu.roll(first, BS - width, 1), second))

    def prepare(a):
        loads[a].wait()

        def body(m, _):
            v = [S32[a, 4 * m + n] * PM[4 * m + n][a:a + 1, :] for n in range(4)]
            v[0], v[2] = swap_lanes(low_half, 64, v[0], v[2])
            v[1], v[3] = swap_lanes(low_half, 64, v[1], v[3])
            v[0], v[1] = swap_lanes(low_quarter, 32, v[0], v[1])
            v[2], v[3] = swap_lanes(low_quarter, 32, v[2], v[3])
            at = pl.multiple_of(m * BS, BS)
            for xx in range(4):
                high, low = split(v[xx])
                Shi[xx, pl.ds(a * BS, BS), pl.ds(at, BS)] = high
                Slo[xx, pl.ds(a * BS, BS), pl.ds(at, BS)] = low
            return 0

        lax.fori_loop(0, 6, body, 0)

    groups = (x, xm, xp, x2)

    def multiply(k, g):
        xx = groups[g]
        ref = group(2 * k + 1 - c, xx)
        rcopy(ref, ref, fs.at[0, 0], fr.at[k, xx], sibling).wait_recv()
        mirror(k, xx)
        for u in range(2):
            part = G[2 * k + u, :, :, pl.ds(pl.multiple_of(xx * 32, 32), 32), :].reshape(6 * BS, BS)
            high, low = split(part)
            Lhi[:, u * BS:(u + 1) * BS] = high
            Llo[:, u * BS:(u + 1) * BS] = low
        for b in range(2):
            rows = slice(384 * b, 384 * b + 384)
            total = jnp.dot(Shi[xx, rows], Lhi[...], preferred_element_type=F32)
            total += jnp.dot(Shi[xx, rows], Llo[...], preferred_element_type=F32)
            total += jnp.dot(Slo[xx, rows], Lhi[...], preferred_element_type=F32)
            for u in range(2):
                part = total[:, u * BS:(u + 1) * BS]
                if g == 0:
                    O[k, u, rows] = part
                else:
                    O[k, u, rows] += part

    is_root = jnp.logical_and(y == h, zl == c)

    def mirror_rows(xx):
        return pl.ds(pl.multiple_of(xx * 32, 32), 32)

    def mirror_copy(k, u, xx):
        return rcopy(G.at[2 * k + u, :, x, mirror_rows(xx)], MIR.at[:, mirror_rows(xx)], ms.at[k, u, xx], mr.at[xx],
                     (row, 2 * k + u))

    def mirror(k, xx):
        for u in range(2):
            mine = col == 2 * k + u

            @pl.when(jnp.logical_and(is_root, jnp.logical_not(mine)))
            def _():
                mirror_copy(k, u, xx).start()

            @pl.when(jnp.logical_and(is_root, mine))
            def _():
                MIR[:, mirror_rows(xx)] = G[2 * k + u, :, x, mirror_rows(xx)]

    def rows_of(yy):
        return pl.ds(pl.multiple_of(yy * SLICE, SLICE), SLICE)

    def scatter_y(k):
        for d in (2, 1, 3):
            yy = (y + d) % 4
            go(rcopy(O.at[k, :, rows_of(yy)], YR.at[k, y], ys.at[k, d - 1], yr.at[k, y], dev(yy=yy)))

    def finish_y(k):
        total = O[k, :, rows_of(y)]
        for d in (1, 3, 2):
            yy = (y + d) % 4
            rcopy(YR.at[k, yy], YR.at[k, yy], ys.at[0, 0], yr.at[k, yy], sibling).wait_recv()
            total += YR[k, yy]
        T[k] = total
        go(rcopy(T.at[k, 1 - zl], ZR.at[k], ws.at[k], wr.at[k], dev(zz=1 - zl)))

    def gather_copy(k):
        return rcopy(FB.at[k], XB.at[rows_of(y)], gs.at[k], gr.at[y], dev(yy=k))

    def finish_z(k):
        rcopy(ZR.at[k], ZR.at[k], ws.at[0], wr.at[k], sibling).wait_recv()
        total = T[k, zl] + ZR[k]

        @pl.when(y == k)
        def _():
            XB[rows_of(y)] = total

        @pl.when(y != k)
        def _():
            FB[k] = total
            gather_copy(k).start()

    def nothing():
        pass

    def fill(k):
        return [lambda g=g: multiply(k, g) for g in range(4)]

    for k in range(NCHUNK):
        assemble(k)
        if k < 2:
            send_z(k)
            send_x(k, 0)
    prepare(0)
    prepare(1)
    stage_z(0)
    send_z(2)
    send_x(2, 0)
    prepare(2)
    stage_z(1)
    stage_x(0, [lambda a=a: prepare(a) for a in (3, 4, 5)] + [nothing])
    send_z(3)
    send_x(3, 0)
    stage_z(2)
    stage_far(0)
    stage_x(1, fill(0))
    scatter_y(0)
    stage_z(3)
    stage_far(1)
    stage_x(2, fill(1))
    scatter_y(1)
    finish_y(0)
    stage_far(2)
    stage_x(3, fill(2))
    scatter_y(2)
    finish_y(1)
    finish_z(0)
    multiply(3, 0)
    multiply(3, 1)
    multiply(3, 2)
    stage_far(3)
    multiply(3, 3)
    scatter_y(3)
    finish_z(1)
    finish_y(2)
    finish_y(3)
    finish_z(2)
    finish_z(3)

    @pl.when(jnp.logical_not(is_root))
    def _():
        for xx in range(4):
            ref = MIR.at[:, mirror_rows(xx)]
            rcopy(ref, ref, ms.at[0, 0, 0], mr.at[xx], sibling).wait_recv()

    for d in (1, 3, 2):
        yy = (y + d) % 4
        rcopy(XB.at[rows_of(yy)], XB.at[rows_of(yy)], gs.at[0], gr.at[yy], sibling).wait_recv()
    full = jnp.zeros((BS, BS), F32)
    for a in range(RBL):
        value = -XB[a * BS:(a + 1) * BS] * RM[a:a + 1, :]
        solved[a, 0] = value
        vhi, vlo = split(value)
        mhi, mlo = split(MIR[a])
        full += lax.dot_general(mhi, vhi, TN, preferred_element_type=F32)
        full += lax.dot_general(mhi, vlo, TN, preferred_element_type=F32)
        full += lax.dot_general(mlo, vhi, TN, preferred_element_type=F32)
    packed = jnp.where(iota((64, BS), 1) < 64, full[:64], full[64:])

    DP[...] = packed
    copy = rcopy(DP, DA, ds_s.at[0], ds_r.at[0], sibling)
    go(copy)
    copy.wait_recv()
    DX[x] = DP[...] + DA[...]
    for d in (2, 1, 3):
        go(rcopy(DX.at[x], DX.at[x], ds_s.at[d], ds_r.at[1 + x], dev(xx=(x + d) % 4)))
    for d in (1, 2, 3):
        xx = (x + d) % 4
        rcopy(DX.at[xx], DX.at[xx], ds_s.at[0], ds_r.at[1 + xx], sibling).wait_recv()
    DH[h] = DX[0] + DX[1] + DX[2] + DX[3]
    for d in (2, 1, 3):
        go(rcopy(DH.at[h], DH.at[h], ds_s.at[3 + d], ds_r.at[5 + h], dev(hh=(h + d) % 4)))
    for d in (1, 2, 3):
        hh = (h + d) % 4
        rcopy(DH.at[hh], DH.at[hh], ds_s.at[0], ds_r.at[5 + hh], sibling).wait_recv()
    total = DH[0] + DH[1] + DH[2] + DH[3]
    diag_out[0] = diag[0] - total[:, :64]
    diag_out[1] = diag[1] - total[:, 64:]

    for copy in sends:
        copy.wait_send()
    for k in range(NCHUNK):
        @pl.when(y != k)
        def _():
            gather_copy(k).wait_send()

        for u in range(2):
            @pl.when(jnp.logical_and(is_root, col != 2 * k + u))
            def _():
                for xx in range(4):
                    mirror_copy(k, u, xx).wait_send()


def finish(rows, diag, rows_out, diag_out):
    rows_out[...] = rows[...]
    diag_out[...] = diag[...]


def local(ancestor_inverse, block_pattern, ancestor_lists, panel, diag_term):
    vmem = pl.BlockSpec(memory_space=pltpu.VMEM)
    dma = pltpu.SemaphoreType.DMA
    shapes = (jax.ShapeDtypeStruct((RBL, 1, BS, BS), F32), jax.ShapeDtypeStruct((2, 64, 64), F32))
    rows, diag = pl.pallas_call(
        kernel,
        out_shape=shapes,
        in_specs=[vmem, pl.BlockSpec(memory_space=pl.ANY), vmem, vmem, vmem],
        out_specs=(vmem, vmem),
        scratch_shapes=[
            pltpu.VMEM((8, 6, 4, BS, BS), F32),
            pltpu.VMEM((NCHUNK, CBL, 4, BS), F32),
            pltpu.VMEM((RBL, CBL, BS, BS), F32),
            pltpu.VMEM((4, RBL * BS, 6 * BS), BF16),
            pltpu.VMEM((4, RBL * BS, 6 * BS), BF16),
            pltpu.VMEM((6 * BS, 2 * BS), BF16),
            pltpu.VMEM((6 * BS, 2 * BS), BF16),
            pltpu.VMEM((NCHUNK, 2, RBL * BS, BS), F32),
            pltpu.VMEM((NCHUNK, NY, 2, SLICE, BS), F32),
            pltpu.VMEM((NCHUNK, 2, SLICE, BS), F32),
            pltpu.VMEM((NCHUNK, SLICE, BS), F32),
            pltpu.VMEM((NCHUNK, SLICE, BS), F32),
            pltpu.VMEM((RBL * BS, BS), F32),
            pltpu.VMEM((RBL, BS, BS), F32),
            pltpu.VMEM((8, 32, BS), F32),
            pltpu.VMEM((8, BS), F32),
            pltpu.VMEM((CBL, 8, BS), F32),
            pltpu.VMEM((64, BS), F32),
            pltpu.VMEM((64, BS), F32),
            pltpu.VMEM((NX, 64, BS), F32),
            pltpu.VMEM((NH, 64, BS), F32),
            dma((RBL,)),
            dma((NCHUNK,)), dma((NCHUNK,)),
            dma((NCHUNK, NX, NH)),
            dma((NCHUNK, 3)),
            dma((NCHUNK, NH, 2)),
            dma((NCHUNK, NH)),
            dma((NCHUNK, NX)), dma((NCHUNK, NX)),
            dma((NCHUNK, 3)), dma((NCHUNK, NY)),
            dma((NCHUNK,)), dma((NCHUNK,)),
            dma((NCHUNK,)), dma((NY,)),
            dma((NCHUNK, 2, 4)), dma((4,)),
            dma((8,)), dma((10,)),
        ],
        compiler_params=pltpu.CompilerParams(collective_id=0, has_side_effects=True,
                                             vmem_limit_bytes=56 * 1024 * 1024),
    )(panel[:, 0], ancestor_inverse, block_pattern, ancestor_lists, diag_term)
    return pl.pallas_call(finish, out_shape=shapes, in_specs=[vmem, vmem], out_specs=(vmem, vmem))(rows, diag)


def solution(mesh):
    placed = (
        P(None, "row", None, "col", None, None),
        P(),
        P(),
        P(None, "col", "row", None),
        P("col", None, None),
    )
    return jax.shard_map(
        local,
        mesh=mesh,
        in_specs=placed,
        out_specs=(P(None, "row", None, "col"), P("col", None, None)),
        check_vma=False,
    )
```
